128 devices in a mesh: row: 16 (over z, y), col: 8 (over x, core).
Axes of the slice: x: 4, y: 4, z: 4, core: 2. Of those that a mesh axis runs over, the one named last changes fastest.
Arguments:
- momentum: float32 [8192, 8192], P('row', 'col'), may hold values from -6 to 6
- gradient: bfloat16 [8192, 8192], P('row', 'col'), may hold values from -6 to 6
- weight: bfloat16 [8192, 8192], P('row', 'col'), may hold values from -6 to 6
- right_start: float32 [8192, 512], P('col', 'row'), may hold values from -0.0625 to 0.0625
Outputs:
- new_momentum: float32 [8192, 8192], P('row', 'col')
- new_weight: bfloat16 [8192, 8192], P('row', 'col')
- new_right: float32 [8192, 512], P('col', 'row')
The draws below stay inside these ranges and needn't reach their ends.
All inputs are finite; a program needn't handle non-finite values.
Results may differ from the reference program's by a relative error of at most 0.001.
Values sent between devices are 32-bit elements; how exact they have to be, the bound alone decides.
No kernel may reach another device: no remote copies, remote signals or barrier semaphores. Data moves between devices by JAX's collectives and lax.ppermute only.
A program may use at most 64 MiB of HBM per device.

```python
import jax
import jax.numpy as jnp
from jax import lax

OUT_DIM = 8192
IN_DIM = 8192
RANK = 512
ITERS = 2


def levels(key, dims, shards, least, top_value):
    loudness = 1.0
    for axis_at, blocks in shards:
        steps = jax.random.uniform(jax.random.fold_in(jax.random.fold_in(key, 6), axis_at), (blocks,), jnp.float32, least / len(shards), top_value / len(shards))
        loudness = loudness * jnp.repeat(jnp.exp(steps), dims[axis_at] // blocks).reshape((-1,) + (1,) * (len(dims) - 1 - axis_at))
    return loudness


def noise(key, dims, spread, most, split=(), held_as=jnp.bfloat16):
    factor_of = levels(key, dims, split, -0.22, 0.18) if split else 1.0
    result = jax.random.normal(key, dims, jnp.float32) * spread * factor_of
    return jnp.minimum(jnp.maximum(result, -most), most).astype(held_as)


def setup_inputs(seed: int = 0) -> dict:
    arg_keys = jax.random.split(jax.random.key(seed), 5)
    return {
        "momentum": noise(arg_keys[0], (OUT_DIM, IN_DIM), 1.0, 6.0, ((0, 16), (1, 8)), jnp.float32),
        "gradient": noise(arg_keys[1], (OUT_DIM, IN_DIM), 1.0, 6.0, ((0, 16), (1, 8))),
        "weight": noise(arg_keys[2], (OUT_DIM, IN_DIM), 1.0, 6.0, ((0, 16), (1, 8))),
        "right_start": noise(arg_keys[3], (IN_DIM, RANK), IN_DIM ** -0.5, 0.0625, ((0, 8), (1, 16)), jnp.float32),
    }


precise_mode = lax.Precision.HIGHEST
momentum_decay = 0.9
step_rate = 0.1
epsilon = 1e-06

def orthonormal(partials):
    gram_sum = jnp.dot(partials.T, partials, precision=precise_mode)
    triangle = jnp.linalg.cholesky(gram_sum)
    return jax.scipy.linalg.solve_triangular(triangle, partials.T, lower=True).T

def reference(momentum, gradient, weight, right_start):
    blended = momentum + gradient.astype(jnp.float32)
    right_factor = right_start
    for iteration in range(ITERS):
        left_rows = orthonormal(jnp.dot(blended, right_factor, precision=precise_mode))
        products = jnp.dot(left_rows.T, blended, precision=precise_mode).T
        col_norms = jnp.sqrt(lax.optimization_barrier(jnp.sum(products * products, axis=0, keepdims=True)) + epsilon)
        right_factor = products / col_norms
    new_momentum = blended - (1.0 - momentum_decay) * jnp.dot(left_rows, products.T, precision=precise_mode)
    scale_factor = step_rate * (OUT_DIM * IN_DIM / RANK) ** 0.5
    update = jnp.dot(left_rows, right_factor.T, precision=precise_mode)
    new_weight = (weight.astype(jnp.float32) - scale_factor * update).astype(jnp.bfloat16)
    return (new_momentum, new_weight, right_factor)
```

```python
import jax
import jax.numpy as jnp
from jax import lax
from jax.experimental import pallas as pl
from jax.experimental.pallas import tpu as pltpu
from jax.sharding import Mesh
from jax.sharding import PartitionSpec as P

OUT_DIM = 8192
IN_DIM = 8192
RANK = 512
ITERS = 2
ROW = ("row_0", "row_1")
COL = ("col_0", "col_1")
X, CORE = COL

precise_mode = lax.Precision.HIGHEST
momentum_decay = 0.9
step_rate = 0.1
epsilon = 1e-06

SWAP = [(0, 1), (1, 0)]
PAIRS_A = [(0, 1), (1, 0), (2, 3), (3, 2)]
PAIRS_B = [(0, 3), (3, 0), (1, 2), (2, 1)]
BLK = 128


def eliminate(d):
    n = BLK // 8
    row = lax.broadcasted_iota(jnp.int32, (BLK, BLK), 0)
    col = lax.broadcasted_iota(jnp.int32, (BLK, BLK), 1)
    eye = jnp.where(row == col, 1.0, 0.0)
    a = [d[8 * g : 8 * g + 8] for g in range(n)]
    x = [eye[8 * g : 8 * g + 8] for g in range(n)]
    sub = lax.broadcasted_iota(jnp.int32, (8, BLK), 0)
    for j in range(BLK):
        gj, s = divmod(j, 8)
        pa = jnp.broadcast_to(a[gj][s : s + 1], (8, BLK))
        px = jnp.broadcast_to(x[gj][s : s + 1], (8, BLK))
        inverse = 1.0 / jnp.broadcast_to(pa[:, j : j + 1], (8, BLK))
        for g in range(gj, n):
            f = jnp.broadcast_to(a[g][:, j : j + 1], (8, BLK)) * inverse
            if g == gj:
                if s == 7:
                    continue
                f = jnp.where(sub > s, f, 0.0)
            a[g] = a[g] - f * pa
            x[g] = x[g] - f * px
    pivots = jnp.sum(jnp.where(row == col, jnp.concatenate(a, 0), 0.0), axis=1, keepdims=True)
    return jnp.concatenate(x, 0) * (1.0 / jnp.sqrt(pivots))


def factor_kernel(gram_ref, out_ref, work_ref):
    n = gram_ref.shape[0]
    work_ref[:, :n] = gram_ref[...]
    r = lax.broadcasted_iota(jnp.int32, (n, n), 0)
    c = lax.broadcasted_iota(jnp.int32, (n, n), 1)
    work_ref[:, n:] = jnp.where(r == c, 1.0, 0.0)

    def block(k, carry):
        at = pl.multiple_of(k * BLK, BLK)
        rows = pl.ds(at, BLK)
        inv = eliminate(work_ref[rows, rows])
        work_ref[rows, :] = jnp.dot(inv, work_ref[rows, :], precision=precise_mode)

        def trailing(i, carry):
            below = pl.ds(pl.multiple_of(i * BLK, BLK), BLK)
            change = lax.dot_general(
                work_ref[rows, below], work_ref[rows, :], (((0,), (0,)), ((), ())), precision=precise_mode
            )
            work_ref[below, :] = work_ref[below, :] - change
            return carry

        lax.fori_loop(k + 1, n // BLK, trailing, 0)
        return carry

    lax.fori_loop(0, n // BLK, block, 0)
    out_ref[...] = work_ref[:, n:]


def inverse_factor(gram):
    n = gram.shape[0]
    return pl.pallas_call(
        factor_kernel,
        out_shape=jax.ShapeDtypeStruct((n, n), jnp.float32),
        scratch_shapes=[pltpu.VMEM((n, 2 * n), jnp.float32)],
        name="inverse_factor",
    )(gram)


def exchange(tiles, axes):
    return lax.all_to_all(tiles, axes, 0, 0, tiled=True)


def gathered(tile, axes):
    size = lax.axis_size(axes)
    tiles = exchange(jnp.broadcast_to(tile[None], (size, *tile.shape)), axes)
    return tiles.reshape(size * tile.shape[0], tile.shape[1])


def both_cores(half):
    other = lax.ppermute(half, CORE, SWAP)
    first = lax.axis_index(CORE) == 0
    return jnp.concatenate([jnp.where(first, half, other), jnp.where(first, other, half)], 0)


def sum_over_x(a, b):
    a, b = a + lax.ppermute(a, X, PAIRS_A), b + lax.ppermute(b, X, PAIRS_B)
    return a + lax.ppermute(a, X, PAIRS_B), b + lax.ppermute(b, X, PAIRS_A)


def sum_over_col(x, extra=None):
    core = lax.axis_index(CORE)
    half = x.shape[0] // 2
    mine = lax.dynamic_slice_in_dim(x, core * half, half, 0)
    theirs = lax.dynamic_slice_in_dim(x, (1 - core) * half, half, 0)
    mine = mine + lax.ppermute(theirs, CORE, SWAP)
    a, b = mine[: half // 2], mine[half // 2 :]
    if extra is not None:
        extra = extra + lax.ppermute(extra, CORE, SWAP)
        a = jnp.concatenate([a, extra], 0)
    a, b = sum_over_x(a, b)
    whole = both_cores(jnp.concatenate([a[: half // 2], b], 0))
    return whole, a[half // 2 :]


def column_squares(x):
    return jnp.sum((x * x).reshape(-1, 8, x.shape[1]), axis=0)


def norms_of(squares):
    return jnp.sqrt(jnp.sum(squares, axis=0, keepdims=True) + epsilon)


def dot(x, y, dims):
    return lax.dot_general(x, y, (dims, ((), ())), precision=precise_mode)


def shards(momentum, gradient, weight, right_start):
    blended = momentum + gradient.astype(jnp.float32)
    right_rows = gathered(right_start.T, ROW)
    total, _ = sum_over_col(dot(blended, right_rows, ((1,), (1,))))
    partials = total
    size = lax.axis_size(ROW)
    core = lax.axis_index(CORE)
    for iteration in range(ITERS):
        raw = dot(blended, partials, ((0,), (0,)))
        half = RANK // 2
        mine = lax.dynamic_slice_in_dim(partials, core * half, half, 1)
        gram_half = dot(mine, partials, ((0,), (0,)))
        raw_rows = raw.shape[0] // size
        both = jnp.concatenate([raw.reshape(size, -1, RANK), gram_half.reshape(size, -1, RANK)], 1)
        summed = jnp.sum(exchange(both, ROW), axis=0)
        gram = both_cores(gathered(summed[raw_rows:], ROW))
        raw_full = gathered(summed[:raw_rows], ROW)
        inverse = inverse_factor(gram)
        products = dot(raw_full, inverse, ((1,), (1,)))
        squares = column_squares(products)
        if iteration + 1 < ITERS:
            total, squares = sum_over_col(dot(blended, products, ((1,), (0,))), squares)
            partials = total / norms_of(squares)
    squares = squares + lax.ppermute(squares, CORE, SWAP)
    squares = squares + lax.ppermute(squares, X, PAIRS_A)
    squares = squares + lax.ppermute(squares, X, PAIRS_B)
    norms = norms_of(squares)
    left = dot(partials, inverse, ((1,), (1,)))
    feedback = dot(left, products, ((1,), (1,)))
    new_momentum = blended - (1.0 - momentum_decay) * feedback
    right_full = products / norms
    width = right_start.shape[1]
    new_right = lax.dynamic_slice_in_dim(right_full, lax.axis_index(ROW) * width, width, 1)
    scale_factor = step_rate * (OUT_DIM * IN_DIM / RANK) ** 0.5
    update = dot(left, right_full, ((1,), (1,)))
    new_weight = (weight.astype(jnp.float32) - scale_factor * update).astype(jnp.bfloat16)
    return (new_momentum, new_weight, new_right)


def solution(mesh):
    finer = Mesh(mesh.devices.reshape(4, 4, 4, 2), ("row_0", "row_1", "col_0", "col_1"))
    placed = (P(ROW, COL), P(ROW, COL), P(ROW, COL), P(COL, ROW))
    return jax.shard_map(
        shards,
        mesh=finer,
        in_specs=placed,
        out_specs=(P(ROW, COL), P(ROW, COL), P(COL, ROW)),
        check_vma=False,
    )
```

```python
import jax
import jax.numpy as jnp
from jax import lax
from jax.experimental import pallas as pl
from jax.experimental.pallas import tpu as pltpu
from jax.sharding import Mesh
from jax.sharding import PartitionSpec as P

OUT_DIM = 8192
IN_DIM = 8192
RANK = 512
ITERS = 2
ROW = ("row_0", "row_1")
COL = ("col_0", "col_1")
X, CORE = COL

precise_mode = lax.Precision.HIGHEST
momentum_decay = 0.9
step_rate = 0.1
epsilon = 1e-06

SWAP = [(0, 1), (1, 0)]
PAIRS_A = [(0, 1), (1, 0), (2, 3), (3, 2)]
PAIRS_B = [(0, 3), (3, 0), (1, 2), (2, 1)]
BLK = 128


def over_lanes(v, j):
    return jnp.broadcast_to(v[:, j : j + 1], v.shape)


def over_sublanes(v, s):
    return jnp.broadcast_to(v[s : s + 1], v.shape)


def eliminate(d):
    n = BLK // 8
    row = lax.broadcasted_iota(jnp.int32, (BLK, BLK), 0)
    col = lax.broadcasted_iota(jnp.int32, (BLK, BLK), 1)
    eye = jnp.where(row == col, 1.0, 0.0)
    a = [d[8 * g : 8 * g + 8] for g in range(n)]
    x = [eye[8 * g : 8 * g + 8] for g in range(n)]
    sub = lax.broadcasted_iota(jnp.int32, (8, BLK), 0)
    out = []
    for g in range(n):
        columns = {h: [over_lanes(a[h], 8 * g + j) for j in range(8)] for h in range(g, n)}
        inverses = jnp.zeros((8, BLK), jnp.float32)
        for s in range(8):
            inverse = 1.0 / over_sublanes(columns[g][s], s)
            inverses = jnp.where(sub == s, inverse, inverses)
            pivot = {j: over_sublanes(columns[g][j], s) for j in range(s + 1, 8)}
            pa, px = over_sublanes(a[g], s), over_sublanes(x[g], s)
            for h in range(g, n):
                if h == g and s == 7:
                    continue
                f = columns[h][s] * inverse
                if h == g:
                    f = jnp.where(sub > s, f, 0.0)
                for j in range(s + 1, 8):
                    columns[h][j] = columns[h][j] - f * pivot[j]
                a[h] = a[h] - f * pa
                x[h] = x[h] - f * px
        out.append(x[g] * jnp.sqrt(inverses))
    return jnp.concatenate(out, 0)


def factor_kernel(gram_ref, out_ref, work_ref):
    n = gram_ref.shape[0]
    work_ref[:, :n] = gram_ref[...]
    r = lax.broadcasted_iota(jnp.int32, (n, n), 0)
    c = lax.broadcasted_iota(jnp.int32, (n, n), 1)
    work_ref[:, n:] = jnp.where(r == c, 1.0, 0.0)

    def block(k, carry):
        at = pl.multiple_of(k * BLK, BLK)
        rows = pl.ds(at, BLK)
        inv = eliminate(work_ref[rows, rows])
        work_ref[rows, :] = jnp.dot(inv, work_ref[rows, :], precision=precise_mode)

        def trailing(i, carry):
            below = pl.ds(pl.multiple_of(i * BLK, BLK), BLK)
            change = lax.dot_general(
                work_ref[rows, below], work_ref[rows, :], (((0,), (0,)), ((), ())), precision=precise_mode
            )
            work_ref[below, :] = work_ref[below, :] - change
            return carry

        lax.fori_loop(k + 1, n // BLK, trailing, 0)
        return carry

    lax.fori_loop(0, n // BLK, block, 0)
    out_ref[...] = work_ref[:, n:]


def inverse_factor(gram):
    n = gram.shape[0]
    return pl.pallas_call(
        factor_kernel,
        out_shape=jax.ShapeDtypeStruct((n, n), jnp.float32),
        scratch_shapes=[pltpu.VMEM((n, 2 * n), jnp.float32)],
        name="inverse_factor",
    )(gram)


def exchange(tiles, axes):
    return lax.all_to_all(tiles, axes, 0, 0, tiled=True)


def gathered(tile, axes):
    size = lax.axis_size(axes)
    tiles = exchange(jnp.broadcast_to(tile[None], (size, *tile.shape)), axes)
    return tiles.reshape(size * tile.shape[0], tile.shape[1])


def both_cores(half):
    other = lax.ppermute(half, CORE, SWAP)
    first = lax.axis_index(CORE) == 0
    return jnp.concatenate([jnp.where(first, half, other), jnp.where(first, other, half)], 0)


def sum_over_x(a, b):
    a, b = a + lax.ppermute(a, X, PAIRS_A), b + lax.ppermute(b, X, PAIRS_B)
    return a + lax.ppermute(a, X, PAIRS_B), b + lax.ppermute(b, X, PAIRS_A)


def sum_over_col(x, extra=None):
    core = lax.axis_index(CORE)
    half = x.shape[0] // 2
    mine = lax.dynamic_slice_in_dim(x, core * half, half, 0)
    theirs = lax.dynamic_slice_in_dim(x, (1 - core) * half, half, 0)
    mine = mine + lax.ppermute(theirs, CORE, SWAP)
    a, b = mine[: half // 2], mine[half // 2 :]
    if extra is not None:
        extra = extra + lax.ppermute(extra, CORE, SWAP)
        a = jnp.concatenate([a, extra], 0)
    a, b = sum_over_x(a, b)
    whole = both_cores(jnp.concatenate([a[: half // 2], b], 0))
    return whole, a[half // 2 :]


def column_squares(x):
    return jnp.sum((x * x).reshape(-1, 8, x.shape[1]), axis=0)


def norms_of(squares):
    return jnp.sqrt(jnp.sum(squares, axis=0, keepdims=True) + epsilon)


def dot(x, y, dims):
    return lax.dot_general(x, y, (dims, ((), ())), precision=precise_mode)


def shards(momentum, gradient, weight, right_start):
    blended = momentum + gradient.astype(jnp.float32)
    right_rows = gathered(right_start.T, ROW)
    total, _ = sum_over_col(dot(blended, right_rows, ((1,), (1,))))
    partials = total
    size = lax.axis_size(ROW)
    core = lax.axis_index(CORE)
    for iteration in range(ITERS):
        raw = dot(blended, partials, ((0,), (0,)))
        half = RANK // 2
        mine = lax.dynamic_slice_in_dim(partials, core * half, half, 1)
        gram_half = dot(mine, partials, ((0,), (0,)))
        raw_rows = raw.shape[0] // size
        both = jnp.concatenate([raw.reshape(size, -1, RANK), gram_half.reshape(size, -1, RANK)], 1)
        summed = jnp.sum(exchange(both, ROW), axis=0)
        gram = both_cores(gathered(summed[raw_rows:], ROW))
        raw_full = gathered(summed[:raw_rows], ROW)
        inverse = inverse_factor(gram)
        products = dot(raw_full, inverse, ((1,), (1,)))
        squares = column_squares(products)
        if iteration + 1 < ITERS:
            total, squares = sum_over_col(dot(blended, products, ((1,), (0,))), squares)
            partials = total / norms_of(squares)
    squares = squares + lax.ppermute(squares, CORE, SWAP)
    squares = squares + lax.ppermute(squares, X, PAIRS_A)
    squares = squares + lax.ppermute(squares, X, PAIRS_B)
    norms = norms_of(squares)
    left = dot(partials, inverse, ((1,), (1,)))
    feedback = dot(left, products, ((1,), (1,)))
    new_momentum = blended - (1.0 - momentum_decay) * feedback
    right_full = products / norms
    width = right_start.shape[1]
    new_right = lax.dynamic_slice_in_dim(right_full, lax.axis_index(ROW) * width, width, 1)
    scale_factor = step_rate * (OUT_DIM * IN_DIM / RANK) ** 0.5
    update = dot(left, right_full, ((1,), (1,)))
    new_weight = (weight.astype(jnp.float32) - scale_factor * update).astype(jnp.bfloat16)
    return (new_momentum, new_weight, new_right)


def solution(mesh):
    finer = Mesh(mesh.devices.reshape(4, 4, 4, 2), ("row_0", "row_1", "col_0", "col_1"))
    placed = (P(ROW, COL), P(ROW, COL), P(ROW, COL), P(COL, ROW))
    return jax.shard_map(
        shards,
        mesh=finer,
        in_specs=placed,
        out_specs=(P(ROW, COL), P(ROW, COL), P(COL, ROW)),
        check_vma=False,
    )
```
